32 devices in a mesh: grp: 4 (over x, core), tp: 4 (over z), cores: 2 (over y).
Axes of the slice: x: 2, y: 2, z: 4, core: 2. Of those that a mesh axis runs over, the one named last changes fastest.
Arguments:
- tokens: bfloat16 [4096, 8192], P('grp', ('tp', 'cores')), may hold values from -6 to 6
- gate_up_weight: bfloat16 [8192, 2, 16384], P(None, None, ('tp', 'cores')), may hold values from -0.0625 to 0.0625
- down_factor_pool: bfloat16 [8, 8192, 256], P(('tp', 'cores'), 'grp'), may hold values from -0.0625 to 0.0625
- up_factor_pool: bfloat16 [8, 4, 8, 128, 1024], P(('tp', 'cores'), 'grp'), may hold values from -0.5 to 0.5
- segment_adapters: int32 [4, 3], replicated, may hold values from 0 to 7
- segment_tile_counts: int32 [4, 3], P('grp'), may hold values from 1 to 4, 8 in all within a row
- adapter_pool_rows: int32 [8], replicated, may hold values from 0 to 7, each once
Outputs:
- hidden: bfloat16 [4096, 16384], P('grp', ('tp', 'cores'))
The draws below stay inside these ranges and needn't reach their ends.
Inputs may be any that keep to these rules, and one draw needn't show every extreme that they name: `segment_tile_counts`: each row sums to 8. `adapter_pool_rows`: each pool row appears once.
All inputs are finite; a program needn't handle non-finite values.
Results may differ from the reference program's by a relative error of at most 0.0036.
Values may be sent and summed in bfloat16 or wider, within the bound.
A program may use at most 320 MiB of HBM per device.

```python
import math
import jax
import jax.numpy as jnp
import numpy as np
from jax import lax

MODEL_WIDTH = 8192
FF_W = 16384
ADAPTER_RANK = 128
TOKS = 1024
TILE = 128
SEGS = 3
TOKEN_GROUPS = 4
GROUP_DEVICES = 8
ADAPTER_POOL = 8
HIDDEN_SHARE_3 = 512
N_GRP = 4


def place_ends(values, key, least, largest):
    longest = values.shape.index(max(values.shape))
    spots = []
    for shift in (0, 1):
        where = [jax.random.randint(jax.random.fold_in(key, axis), (), 0, length) for axis, length in enumerate(values.shape)]
        where[longest] = (where[longest] + shift) % values.shape[longest]
        spots.append(tuple(where))
    return values.at[spots[0]].set(least).at[spots[1]].set(largest)


def levels(key, dims, cuts, low, top_value):
    def one(axis_at, shards_of):
        steps = jax.random.uniform(jax.random.fold_in(jax.random.fold_in(key, 6), axis_at), (shards_of,), jnp.float32, low / len(cuts), top_value / len(cuts))
        return jnp.repeat(jnp.exp(steps), dims[axis_at] // shards_of).reshape((-1,) + (1,) * (len(dims) - axis_at - 1))

    level = one(*cuts[0])
    for cut in cuts[1:]:
        level = level * one(*cut)
    return level


def split_up(number_of, total, most, slope):
    weights = [(1 << 20) // math.isqrt(rank ** slope) + 1 for rank in range(2, number_of + 1)]
    surplus, counts = total - most - (number_of - 1), [1] * (number_of - 1)
    while surplus > 0:
        candidates = [i for i in range(number_of - 1) if counts[i] < most]
        pool, budget = sum([weights[i] for i in candidates]), surplus
        for i in candidates:
            extra = min(most - counts[i], max(1, budget * weights[i] // pool), surplus)
            counts[i] = counts[i] + extra
            surplus = surplus - extra
    return np.array([most] + counts)


def uneven(rng, number_of, total, bound, slope):
    if number_of == 2:
        one = jax.random.randint(rng, (), max(1, total - bound), min(bound, total - 1) + 1)
        return jnp.stack([one, total - one])
    lengths = jnp.asarray(split_up(number_of, total, bound, slope), jnp.int32)
    couples = (number_of - 1) // 2
    giver, receiver = lengths[1:1 + 2 * couples:2], lengths[2:2 + 2 * couples:2]
    slack = jnp.minimum(giver - 1, bound - receiver)
    passed = jax.random.randint(jax.random.fold_in(rng, 1), (couples,), 0, 1 << 20) % (slack + 1)
    lengths = lengths.at[1:1 + 2 * couples:2].set(giver - passed).at[2:2 + 2 * couples:2].set(receiver + passed)
    return lengths[jax.random.permutation(jax.random.fold_in(rng, 2), number_of)]


def bell_draw(own_key, dims, scale, reach, cuts=(), kind=jnp.bfloat16):
    values = jax.random.normal(own_key, dims, jnp.float32) * scale
    if len(cuts) > 0:
        values = levels(own_key, dims, cuts, -0.22, 0.18) * values
    return jnp.clip(values, min=-reach, max=reach).astype(kind)


def setup_inputs(seed: int = 0) -> dict:
    seeds = jax.random.split(jax.random.key(seed), 8)
    return {
        "tokens": bell_draw(seeds[0], (TOKEN_GROUPS * TOKS, MODEL_WIDTH), 1.0, 6.0, ((0, 4), (1, 8))),
        "gate_up_weight": bell_draw(seeds[1], (MODEL_WIDTH, 2, FF_W), MODEL_WIDTH ** -0.5, 0.0625, ((2, 8),)),
        "down_factor_pool": bell_draw(seeds[2], (ADAPTER_POOL, MODEL_WIDTH, 2 * ADAPTER_RANK), MODEL_WIDTH ** -0.5, 0.0625, ((0, 8), (1, 4))),
        "up_factor_pool": bell_draw(seeds[3], (ADAPTER_POOL, TOKEN_GROUPS, GROUP_DEVICES, ADAPTER_RANK, 2 * HIDDEN_SHARE_3), ADAPTER_RANK ** -0.5, 0.5, ((0, 8), (1, 4))),
        "segment_adapters": place_ends(jax.random.randint(seeds[4], (TOKEN_GROUPS, SEGS), 0, ADAPTER_POOL), jax.random.fold_in(seeds[4], 1), 0, ADAPTER_POOL - 1).astype(jnp.int32),
        "segment_tile_counts": jax.vmap(lambda own: uneven(own, SEGS, TOKS // TILE, TOKS // TILE // 2, 1))(jax.random.split(seeds[5], TOKEN_GROUPS)).reshape((TOKEN_GROUPS, SEGS)).astype(jnp.int32),
        "adapter_pool_rows": jax.random.permutation(seeds[6], ADAPTER_POOL).astype(jnp.int32),
    }


adapter_scale = 0.5


def reference(tokens, gate_up_weight, down_factor_pool, up_factor_pool, segment_adapters, segment_tile_counts, adapter_pool_rows):
    tile_count = TOKS // TILE
    bounds = jnp.cumsum(segment_tile_counts, axis=1)
    positions = jnp.arange(tile_count, dtype=jnp.int32)
    tile_seg = jnp.sum((bounds[:, None, :] <= positions[None, :, None]).astype(jnp.int32), axis=2).astype(jnp.int32)
    tile_ids = jnp.take_along_axis(segment_adapters, tile_seg, axis=1)
    tile_rows = jnp.take(adapter_pool_rows, tile_ids.reshape(-1)).astype(jnp.int32)
    frozen_output = jnp.dot(tokens, gate_up_weight.reshape(MODEL_WIDTH, 2 * FF_W), preferred_element_type=jnp.float32)
    frozen_output = frozen_output.reshape(N_GRP * TOKS, 2, FF_W)
    token_tiles = tokens.reshape(N_GRP * tile_count, TILE, MODEL_WIDTH)

    def one_tile(item):
        token_rows_block, adapter_pool_row = item
        reduced_input = jnp.dot(token_rows_block, down_factor_pool[adapter_pool_row], preferred_element_type=jnp.float32).astype(jnp.bfloat16)
        expanded_output = up_factor_pool[adapter_pool_row].reshape(N_GRP, GROUP_DEVICES, ADAPTER_RANK, 2, HIDDEN_SHARE_3)
        expanded_output = jnp.transpose(expanded_output, (2, 3, 1, 0, 4)).reshape(ADAPTER_RANK, 2, FF_W)
        gate_part = jnp.dot(reduced_input[:, :ADAPTER_RANK], expanded_output[:, 0, :], preferred_element_type=jnp.float32)
        up_part = jnp.dot(reduced_input[:, ADAPTER_RANK:], expanded_output[:, 1, :], preferred_element_type=jnp.float32)
        return jnp.stack([gate_part, up_part], axis=1)

    adapted_output = lax.map(one_tile, (token_tiles, tile_rows)).reshape(N_GRP * TOKS, 2, FF_W)
    gate_combined = frozen_output[:, 0, :] + adapter_scale * adapted_output[:, 0, :]
    up_combined = frozen_output[:, 1, :] + adapter_scale * adapted_output[:, 1, :]
    return (jax.nn.silu(gate_combined) * up_combined).astype(jnp.bfloat16)
```

```python
import functools

import jax
import jax.numpy as jnp
from jax import lax
from jax.experimental import pallas as pl
from jax.experimental.pallas import tpu as pltpu
from jax.sharding import PartitionSpec as P

TILE = 128
VMEM_LIMIT = 60 * 1024 * 1024

adapter_scale = 0.5

TP = ("tp", "cores")


def tile_segments(tile_lengths, tile_count):
    bounds = jnp.cumsum(tile_lengths)
    positions = jnp.arange(tile_count, dtype=jnp.int32)
    return jnp.sum((bounds[None, :] <= positions[:, None]).astype(jnp.int32), axis=1)


def ring_device(position, tp_size, cores_size):
    c = position // tp_size
    t = position % tp_size
    t = t + (c % 2) * (tp_size - 1 - 2 * t)
    return t * cores_size + c


def ring_position(tp_index, cores_index, tp_size):
    t = tp_index + (cores_index % 2) * (tp_size - 1 - 2 * tp_index)
    return cores_index * tp_size + t


def partial_kernel(count, with_acc, rows_ref, *refs):
    xs, ws = refs[:count], refs[count : 2 * count]
    out = refs[-1]
    for h in range(2):
        total = refs[2 * count][h] if with_acc else None
        for x, w in zip(xs, ws):
            term = jnp.dot(x[...], w[h], preferred_element_type=jnp.float32)
            total = term if total is None else total + term
        out[h] = total


def partial_matmul(xs, weight, rows, acc, block_cols):
    count = len(xs)
    tokens, depth = xs[0].shape
    hidden = weight.shape[2]
    block_rows = tokens // 2
    in_specs = [pl.BlockSpec((block_rows, depth), lambda j, i, r: (i, 0))] * count
    for k in range(count):
        in_specs.append(
            pl.BlockSpec((2, depth, block_cols), lambda j, i, r, k=k: (0, r[k], j))
        )
    acc_spec = pl.BlockSpec((2, block_rows, block_cols), lambda j, i, r: (0, i, j))
    operands = list(xs) + [weight] * count
    aliases = {}
    if acc is not None:
        in_specs.append(acc_spec)
        aliases = {1 + len(operands): 0}
        operands.append(acc)
    return pl.pallas_call(
        functools.partial(partial_kernel, count, acc is not None),
        out_shape=jax.ShapeDtypeStruct((2, tokens, hidden), jnp.float32),
        grid_spec=pltpu.PrefetchScalarGridSpec(
            num_scalar_prefetch=1,
            grid=(hidden // block_cols, 2),
            in_specs=in_specs,
            out_specs=acc_spec,
        ),
        input_output_aliases=aliases,
        compiler_params=pltpu.CompilerParams(vmem_limit_bytes=VMEM_LIMIT),
        cost_estimate=pl.CostEstimate(
            flops=4 * count * tokens * depth * hidden,
            bytes_accessed=count * 4 * depth * hidden + 16 * tokens * hidden,
            transcendentals=0,
        ),
    )(rows, *operands)


def final_kernel(tiles_per_block, rank, rows_ref, seg_ref, x, w, acc, shrunk, b, out, total):
    i = pl.program_id(1)
    narrow = out.shape[1]
    for h in range(2):
        total[h] = acc[h] + jnp.dot(x[...], w[h], preferred_element_type=jnp.float32)

    for t in range(tiles_per_block):
        seg = seg_ref[i * tiles_per_block + t]
        span = slice(t * TILE, (t + 1) * TILE)
        both = []
        for h in range(2):
            delta = jnp.dot(
                shrunk[span, h * rank : (h + 1) * rank],
                b[0, seg, :, h * narrow : (h + 1) * narrow],
                preferred_element_type=jnp.float32,
            )
            both.append(total[h, span] + adapter_scale * delta)
        gate, up = both
        out[span] = (gate / (1.0 + jnp.exp(-gate)) * up).astype(out.dtype)


def final_matmul(x, weight, rows, acc, shrunk, b_chosen, tile_seg):
    tokens, depth = x.shape
    hidden = weight.shape[2]
    blocks, segs, rank, twice = b_chosen.shape
    narrow = twice // 2
    block_rows = tokens // 2
    return pl.pallas_call(
        functools.partial(final_kernel, block_rows // TILE, rank),
        out_shape=jax.ShapeDtypeStruct((tokens, hidden), jnp.bfloat16),
        grid_spec=pltpu.PrefetchScalarGridSpec(
            num_scalar_prefetch=2,
            grid=(blocks, 2),
            in_specs=[
                pl.BlockSpec((block_rows, depth), lambda j, i, r, s: (i, 0)),
                pl.BlockSpec((2, depth, narrow), lambda j, i, r, s: (0, r[0], j)),
                pl.BlockSpec((2, block_rows, narrow), lambda j, i, r, s: (0, i, j)),
                pl.BlockSpec((block_rows, 2 * rank), lambda j, i, r, s: (i, 0)),
                pl.BlockSpec((1, segs, rank, twice), lambda j, i, r, s: (j, 0, 0, 0)),
            ],
            out_specs=pl.BlockSpec((block_rows, narrow), lambda j, i, r, s: (i, j)),
            scratch_shapes=[pltpu.VMEM((2, block_rows, narrow), jnp.float32)],
        ),
        compiler_params=pltpu.CompilerParams(vmem_limit_bytes=VMEM_LIMIT),
        cost_estimate=pl.CostEstimate(
            flops=4 * tokens * (depth + rank) * hidden,
            bytes_accessed=4 * depth * hidden + 10 * tokens * hidden,
            transcendentals=tokens * hidden,
        ),
    )(rows, tile_seg, x, weight, acc, shrunk, b_chosen)


def per_device(
    tokens,
    gate_up_weight,
    down_factor_pool,
    up_factor_pool,
    segment_adapters,
    segment_tile_counts,
    adapter_pool_rows,
):
    groups = lax.axis_size("grp")
    tp_size, cores_size = lax.axis_size("tp"), lax.axis_size("cores")
    n = tp_size * cores_size
    token_count, depth = tokens.shape
    local_hidden_width = gate_up_weight.shape[2]
    twice_rank = down_factor_pool.shape[2]
    narrow = local_hidden_width // groups
    seg_count = segment_adapters.shape[1]
    half = token_count // 2

    me = ring_position(lax.axis_index("tp"), lax.axis_index("cores"), tp_size)
    order = [ring_device(k, tp_size, cores_size) for k in range(n)]
    forward = [(order[k], order[(k + 1) % n]) for k in range(n)]
    backward = [(order[(k + 1) % n], order[k]) for k in range(n)]

    def owner(shift):
        return ring_device((me + shift + n) % n, tp_size, cores_size).astype(jnp.int32)

    full_steps = (n - 1) // 2
    lefts, rights = [tokens], [tokens]
    for _ in range(full_steps):
        lefts.append(lax.ppermute(lefts[-1], TP, forward))
        rights.append(lax.ppermute(rights[-1], TP, backward))
    last = jnp.concatenate(
        [
            lax.ppermute(lefts[-1][:half], TP, forward),
            lax.ppermute(rights[-1][half:], TP, backward),
        ],
        axis=0,
    )

    piece = depth // groups
    a = down_factor_pool.reshape(n // groups, groups, piece, twice_rank)
    a = lax.all_to_all(a, "grp", split_axis=1, concat_axis=0, tiled=True)
    a = a.reshape(n, piece, twice_rank)
    a = lax.all_to_all(a, TP, split_axis=0, concat_axis=0, tiled=True)
    b = up_factor_pool.reshape(up_factor_pool.shape[2:])
    b = lax.all_to_all(b, TP, split_axis=0, concat_axis=0, tiled=True)
    slots = jnp.take(adapter_pool_rows, segment_adapters.reshape(-1))
    a = jnp.take(a, slots, axis=0)
    b = jnp.take(b, slots, axis=0)
    a = lax.all_to_all(a, "grp", split_axis=0, concat_axis=0, tiled=True)
    b = lax.all_to_all(b, "grp", split_axis=0, concat_axis=0, tiled=True)
    a = a.reshape(groups, seg_count, piece, twice_rank)
    b = b.reshape(groups, seg_count, *b.shape[1:])
    block_cols = narrow
    if narrow % 128:
        block_cols = local_hidden_width
        b = b.reshape(groups, seg_count, b.shape[2], 2, narrow)
        b = jnp.transpose(b, (1, 2, 3, 0, 4))
        b = b.reshape(1, seg_count, b.shape[1], 2 * block_cols)

    tile_count = token_count // TILE
    tile_seg = tile_segments(segment_tile_counts[0], tile_count).astype(jnp.int32)
    row_seg = jnp.repeat(tile_seg, TILE)[:, None]
    partial = None
    for j in range(seg_count):
        term = jnp.dot(
            tokens, a[:, j].reshape(depth, twice_rank), preferred_element_type=jnp.float32
        )
        partial = term if partial is None else jnp.where(row_seg == j, term, partial)
    share = token_count // n
    partial = lax.all_to_all(
        partial.reshape(n, share, twice_rank), TP, split_axis=0, concat_axis=0, tiled=True
    )
    own = jnp.sum(partial, axis=0).astype(jnp.bfloat16)
    shrunk = lax.all_to_all(
        jnp.broadcast_to(own[None], (n, share, twice_rank)),
        TP,
        split_axis=0,
        concat_axis=0,
        tiled=True,
    ).reshape(token_count, twice_rank)

    weight = jnp.transpose(gate_up_weight, (1, 0, 2))
    acc = None
    for s in range(1, full_steps + 1):
        xs = [lefts[s], rights[s]]
        rows = [owner(-s), owner(s)]
        if s == 1:
            xs.insert(0, tokens)
            rows.insert(0, owner(0))
        acc = partial_matmul(xs, weight, jnp.stack(rows), acc, block_cols)
    return final_matmul(
        last, weight, jnp.stack([owner(n // 2)]), acc, shrunk, b, tile_seg
    )


def solution(mesh):
    return jax.shard_map(
        per_device,
        mesh=mesh,
        in_specs=(
            P("grp", ("tp", "cores")),
            P(None, None, ("tp", "cores")),
            P(("tp", "cores"), "grp", None),
            P(("tp", "cores"), "grp", None, None, None),
            P(),
            P("grp", None),
            P(),
        ),
        out_specs=P("grp", ("tp", "cores")),
        check_vma=False,
    )
```

```python
import functools

import jax
import jax.numpy as jnp
from jax import lax
from jax.experimental import pallas as pl
from jax.experimental.pallas import tpu as pltpu
from jax.sharding import PartitionSpec as P


TILE = 128
VMEM_LIMIT = 60 * 1024 * 1024

adapter_scale = 0.5

TP = ("tp", "cores")


def tile_segments(tile_lengths, tile_count):
    bounds = jnp.cumsum(tile_lengths)
    positions = jnp.arange(tile_count, dtype=jnp.int32)
    return jnp.sum((bounds[None, :] <= positions[:, None]).astype(jnp.int32), axis=1)


def ring_device(position, tp_size, cores_size):
    c = position // tp_size
    t = position % tp_size
    t = t + (c % 2) * (tp_size - 1 - 2 * t)
    return t * cores_size + c


def ring_position(tp_index, cores_index, tp_size):
    t = tp_index + (cores_index % 2) * (tp_size - 1 - 2 * tp_index)
    return cores_index * tp_size + t


def partial_kernel(count, with_acc, rows_ref, *refs):
    xs, ws = refs[:count], refs[count : 2 * count]
    out = refs[-1]
    for h in range(2):
        total = refs[2 * count][h] if with_acc else None
        for x, w in zip(xs, ws):
            term = jnp.dot(x[...], w[h], preferred_element_type=jnp.float32)
            total = term if total is None else total + term
        out[h] = total


def partial_matmul(xs, weight, rows, acc, block_cols):
    count = len(xs)
    tokens, depth = xs[0].shape
    hidden = weight.shape[2]
    block_cols = min(block_cols, 256)
    in_specs = [pl.BlockSpec((tokens, depth), lambda j, r: (0, 0))] * count
    for k in range(count):
        in_specs.append(
            pl.BlockSpec((2, depth, block_cols), lambda j, r, k=k: (0, r[k], j))
        )
    acc_spec = pl.BlockSpec((2, tokens, block_cols), lambda j, r: (0, 0, j))
    operands = list(xs) + [weight] * count
    aliases = {}
    if acc is not None:
        in_specs.append(acc_spec)
        aliases = {1 + len(operands): 0}
        operands.append(acc)
    return pl.pallas_call(
        functools.partial(partial_kernel, count, acc is not None),
        out_shape=jax.ShapeDtypeStruct((2, tokens, hidden), jnp.float32),
        grid_spec=pltpu.PrefetchScalarGridSpec(
            num_scalar_prefetch=1,
            grid=(hidden // block_cols,),
            in_specs=in_specs,
            out_specs=acc_spec,
        ),
        input_output_aliases=aliases,
        compiler_params=pltpu.CompilerParams(vmem_limit_bytes=VMEM_LIMIT),
        cost_estimate=pl.CostEstimate(
            flops=4 * count * tokens * depth * hidden,
            bytes_accessed=count * 4 * depth * hidden + 16 * tokens * hidden,
            transcendentals=0,
        ),
    )(rows, *operands)


def final_kernel(tiles_per_half, rank, rows_ref, seg_ref, xt, xb, w, acc, shrunk, b, out, total):
    narrow = out.shape[1]
    for p, x in enumerate((xt, xb)):
        for h in range(2):
            span = slice(p * x.shape[0], (p + 1) * x.shape[0])
            total[h, span] = acc[h, span] + jnp.dot(
                x[...], w[h], preferred_element_type=jnp.float32
            )
        for t in range(p * tiles_per_half, (p + 1) * tiles_per_half):
            seg = seg_ref[t]
            span = slice(t * TILE, (t + 1) * TILE)
            both = []
            for h in range(2):
                delta = jnp.dot(
                    shrunk[span, h * rank : (h + 1) * rank],
                    b[0, seg, :, h * narrow : (h + 1) * narrow],
                    preferred_element_type=jnp.float32,
                )
                both.append(total[h, span] + adapter_scale * delta)
            gate, up = both
            out[span] = (gate / (1.0 + jnp.exp(-gate)) * up).astype(out.dtype)


def final_matmul(xt, xb, weight, rows, acc, shrunk, b_chosen, tile_seg):
    half, depth = xt.shape
    tokens = 2 * half
    hidden = weight.shape[2]
    blocks, segs, rank, twice = b_chosen.shape
    narrow = twice // 2
    return pl.pallas_call(
        functools.partial(final_kernel, half // TILE, rank),
        out_shape=jax.ShapeDtypeStruct((tokens, hidden), jnp.bfloat16),
        grid_spec=pltpu.PrefetchScalarGridSpec(
            num_scalar_prefetch=2,
            grid=(blocks,),
            in_specs=[
                pl.BlockSpec((half, depth), lambda j, r, s: (0, 0)),
                pl.BlockSpec((half, depth), lambda j, r, s: (0, 0)),
                pl.BlockSpec((2, depth, narrow), lambda j, r, s: (0, r[0], j)),
                pl.BlockSpec((2, tokens, narrow), lambda j, r, s: (0, 0, j)),
                pl.BlockSpec((tokens, 2 * rank), lambda j, r, s: (0, 0)),
                pl.BlockSpec((1, segs, rank, twice), lambda j, r, s: (j, 0, 0, 0)),
            ],
            out_specs=pl.BlockSpec((tokens, narrow), lambda j, r, s: (0, j)),
            scratch_shapes=[pltpu.VMEM((2, tokens, narrow), jnp.float32)],
        ),
        compiler_params=pltpu.CompilerParams(vmem_limit_bytes=VMEM_LIMIT),
        cost_estimate=pl.CostEstimate(
            flops=4 * tokens * (depth + rank) * hidden,
            bytes_accessed=4 * depth * hidden + 10 * tokens * hidden,
            transcendentals=tokens * hidden,
        ),
    )(rows, tile_seg, xt, xb, weight, acc, shrunk, b_chosen)


def compute(
    tokens,
    gate_up_weight,
    down_factor_pool,
    up_factor_pool,
    segment_adapters,
    segment_tile_counts,
    adapter_pool_rows,
):
    groups = lax.axis_size("grp")
    tp_size, cores_size = lax.axis_size("tp"), lax.axis_size("cores")
    n = tp_size * cores_size
    token_count, depth = tokens.shape
    local_hidden_width = gate_up_weight.shape[2]
    twice_rank = down_factor_pool.shape[2]
    narrow = local_hidden_width // groups
    seg_count = segment_adapters.shape[1]
    half = token_count // 2

    me = ring_position(lax.axis_index("tp"), lax.axis_index("cores"), tp_size)
    order = [ring_device(k, tp_size, cores_size) for k in range(n)]
    forward = [(order[k], order[(k + 1) % n]) for k in range(n)]
    backward = [(order[(k + 1) % n], order[k]) for k in range(n)]

    def owner(shift):
        return ring_device((me + shift + n) % n, tp_size, cores_size).astype(jnp.int32)

    full_steps = (n - 1) // 2
    lefts, rights = [tokens], [tokens]
    for _ in range(1, full_steps + 1):
        lefts.append(lax.ppermute(lefts[-1], TP, forward))
        rights.append(lax.ppermute(rights[-1], TP, backward))
    last_top = lax.ppermute(lefts[-1][:half], TP, forward)
    last_bottom = lax.ppermute(rights[-1][half:], TP, backward)

    piece = depth // groups
    a = down_factor_pool.reshape(n // groups, groups, piece, twice_rank)
    a = lax.all_to_all(a, "grp", split_axis=1, concat_axis=0, tiled=True)
    a = a.reshape(n, piece, twice_rank)
    a = lax.all_to_all(a, TP, split_axis=0, concat_axis=0, tiled=True)
    b = up_factor_pool.reshape(up_factor_pool.shape[2:])
    b = lax.all_to_all(b, TP, split_axis=0, concat_axis=0, tiled=True)
    slots = jnp.take(adapter_pool_rows, segment_adapters.reshape(-1))
    a = jnp.take(a, slots, axis=0)
    b = jnp.take(b, slots, axis=0)
    a = lax.all_to_all(a, "grp", split_axis=0, concat_axis=0, tiled=True)
    b = lax.all_to_all(b, "grp", split_axis=0, concat_axis=0, tiled=True)
    a = a.reshape(groups, seg_count, piece, twice_rank)
    b = b.reshape(groups, seg_count, *b.shape[1:])
    block_cols = narrow
    if narrow % 128:
        block_cols = local_hidden_width
        b = b.reshape(groups, seg_count, b.shape[2], 2, narrow)
        b = jnp.transpose(b, (1, 2, 3, 0, 4))
        b = b.reshape(1, seg_count, b.shape[1], 2 * block_cols)

    tile_count = token_count // TILE
    tile_seg = tile_segments(segment_tile_counts[0], tile_count).astype(jnp.int32)
    row_seg = jnp.repeat(tile_seg, TILE)[:, None]
    partial = None
    for j in range(seg_count):
        term = jnp.dot(
            tokens, a[:, j].reshape(depth, twice_rank), preferred_element_type=jnp.float32
        )
        partial = term if partial is None else jnp.where(row_seg == j, term, partial)
    share = token_count // n
    partial = lax.all_to_all(
        partial.reshape(n, share, twice_rank), TP, split_axis=0, concat_axis=0, tiled=True
    )
    own = jnp.sum(partial, axis=0).astype(jnp.bfloat16)
    shrunk = lax.all_to_all(
        jnp.broadcast_to(own[None], (n, share, twice_rank)),
        TP,
        split_axis=0,
        concat_axis=0,
        tiled=True,
    ).reshape(token_count, twice_rank)

    weight = jnp.transpose(gate_up_weight, (1, 0, 2))
    acc = None
    for s in range(1, full_steps + 1):
        xs = [lefts[s], rights[s]]
        rows = [owner(-s), owner(s)]
        if s == 1:
            xs.insert(0, tokens)
            rows.insert(0, owner(0))
        acc = partial_matmul(xs, weight, jnp.stack(rows), acc, block_cols)
    return final_matmul(
        last_top, last_bottom, weight, jnp.stack([owner(n // 2)]), acc, shrunk, b, tile_seg
    )


def solution(mesh):
    return jax.shard_map(
        compute,
        mesh=mesh,
        in_specs=(
            P("grp", ("tp", "cores")),
            P(None, None, ("tp", "cores")),
            P(("tp", "cores"), "grp", None),
            P(("tp", "cores"), "grp", None, None, None),
            P(),
            P("grp", None),
            P(),
        ),
        out_specs=P("grp", ("tp", "cores")),
        check_vma=False,
    )
```

```python
import functools

import jax
import jax.numpy as jnp
from jax import lax
from jax.experimental import pallas as pl
from jax.experimental.pallas import tpu as pltpu
from jax.sharding import PartitionSpec as P


TILE = 128
VMEM_LIMIT = 60 * 1024 * 1024

adapter_scale = 0.5

TP = ("tp", "cores")


def tile_segments(tile_lengths, tile_count):
    bounds = jnp.cumsum(tile_lengths)
    positions = jnp.arange(tile_count, dtype=jnp.int32)
    return jnp.sum((bounds[None, :] <= positions[:, None]).astype(jnp.int32), axis=1)


def ring_device(position, tp_size, cores_size):
    c = position // tp_size
    t = position % tp_size
    t = t + (c % 2) * (tp_size - 1 - 2 * t)
    return t * cores_size + c


def ring_position(tp_index, cores_index, tp_size):
    t = tp_index + (cores_index % 2) * (tp_size - 1 - 2 * tp_index)
    return cores_index * tp_size + t


def partial_kernel(count, with_acc, rows_ref, *refs):
    xs, ws = refs[:count], refs[count : 2 * count]
    out = refs[-1]
    ws = [jnp.swapaxes(w[...], 0, 1) for w in ws]
    for h in range(2):
        total = refs[2 * count][h] if with_acc else None
        for x, w in zip(xs, ws):
            term = jnp.dot(x[...], w[h], preferred_element_type=jnp.float32)
            total = term if total is None else total + term
        out[h] = total


def partial_matmul(xs, weight, rows, acc, block_cols):
    count = len(xs)
    tokens, depth = xs[0].shape
    hidden = weight.shape[2]
    block_cols = min(block_cols, 256)
    in_specs = [pl.BlockSpec((tokens, depth), lambda j, r: (0, 0))] * count
    for k in range(count):
        in_specs.append(
            pl.BlockSpec((depth, 2, block_cols), lambda j, r, k=k: (r[k], 0, j))
        )
    acc_spec = pl.BlockSpec((2, tokens, block_cols), lambda j, r: (0, 0, j))
    operands = list(xs) + [weight] * count
    aliases = {}
    if acc is not None:
        in_specs.append(acc_spec)
        aliases = {1 + len(operands): 0}
        operands.append(acc)
    return pl.pallas_call(
        functools.partial(partial_kernel, count, acc is not None),
        out_shape=jax.ShapeDtypeStruct((2, tokens, hidden), jnp.float32),
        grid_spec=pltpu.PrefetchScalarGridSpec(
            num_scalar_prefetch=1,
            grid=(hidden // block_cols,),
            in_specs=in_specs,
            out_specs=acc_spec,
        ),
        input_output_aliases=aliases,
        compiler_params=pltpu.CompilerParams(vmem_limit_bytes=VMEM_LIMIT),
        cost_estimate=pl.CostEstimate(
            flops=4 * count * tokens * depth * hidden,
            bytes_accessed=count * 4 * depth * hidden + 16 * tokens * hidden,
            transcendentals=0,
        ),
    )(rows, *operands)


def final_kernel(tiles_per_half, rank, rows_ref, seg_ref, xt, xb, w, acc, shrunk, b, out, total):
    narrow = out.shape[1]
    w = jnp.swapaxes(w[...], 0, 1)
    for p, x in enumerate((xt, xb)):
        for h in range(2):
            span = slice(p * x.shape[0], (p + 1) * x.shape[0])
            total[h, span] = acc[h, span] + jnp.dot(
                x[...], w[h], preferred_element_type=jnp.float32
            )
        for t in range(p * tiles_per_half, (p + 1) * tiles_per_half):
            seg = seg_ref[t]
            span = slice(t * TILE, (t + 1) * TILE)
            both = []
            for h in range(2):
                delta = jnp.dot(
                    shrunk[span, h * rank : (h + 1) * rank],
                    b[0, seg, :, h * narrow : (h + 1) * narrow],
                    preferred_element_type=jnp.float32,
                )
                both.append(total[h, span] + adapter_scale * delta)
            gate, up = both
            out[span] = (gate / (1.0 + jnp.exp(-gate)) * up).astype(out.dtype)


def final_matmul(xt, xb, weight, rows, acc, shrunk, b_chosen, tile_seg):
    half, depth = xt.shape
    tokens = 2 * half
    hidden = weight.shape[2]
    blocks, segs, rank, twice = b_chosen.shape
    narrow = twice // 2
    return pl.pallas_call(
        functools.partial(final_kernel, half // TILE, rank),
        out_shape=jax.ShapeDtypeStruct((tokens, hidden), jnp.bfloat16),
        grid_spec=pltpu.PrefetchScalarGridSpec(
            num_scalar_prefetch=2,
            grid=(blocks,),
            in_specs=[
                pl.BlockSpec((half, depth), lambda j, r, s: (0, 0)),
                pl.BlockSpec((half, depth), lambda j, r, s: (0, 0)),
                pl.BlockSpec((depth, 2, narrow), lambda j, r, s: (r[0], 0, j)),
                pl.BlockSpec((2, tokens, narrow), lambda j, r, s: (0, 0, j)),
                pl.BlockSpec((tokens, 2 * rank), lambda j, r, s: (0, 0)),
                pl.BlockSpec((1, segs, rank, twice), lambda j, r, s: (j, 0, 0, 0)),
            ],
            out_specs=pl.BlockSpec((tokens, narrow), lambda j, r, s: (0, j)),
            scratch_shapes=[pltpu.VMEM((2, tokens, narrow), jnp.float32)],
        ),
        compiler_params=pltpu.CompilerParams(vmem_limit_bytes=VMEM_LIMIT),
        cost_estimate=pl.CostEstimate(
            flops=4 * tokens * (depth + rank) * hidden,
            bytes_accessed=4 * depth * hidden + 10 * tokens * hidden,
            transcendentals=tokens * hidden,
        ),
    )(rows, tile_seg, xt, xb, weight, acc, shrunk, b_chosen)


def compute(
    tokens,
    gate_up_weight,
    down_factor_pool,
    up_factor_pool,
    segment_adapters,
    segment_tile_counts,
    adapter_pool_rows,
):
    groups = lax.axis_size("grp")
    tp_size, cores_size = lax.axis_size("tp"), lax.axis_size("cores")
    n = tp_size * cores_size
    token_count, depth = tokens.shape
    local_hidden_width = gate_up_weight.shape[2]
    twice_rank = down_factor_pool.shape[2]
    narrow = local_hidden_width // groups
    seg_count = segment_adapters.shape[1]
    half = token_count // 2

    me = ring_position(lax.axis_index("tp"), lax.axis_index("cores"), tp_size)
    order = [ring_device(k, tp_size, cores_size) for k in range(n)]
    forward = [(order[k], order[(k + 1) % n]) for k in range(n)]
    backward = [(order[(k + 1) % n], order[k]) for k in range(n)]

    def owner(shift):
        return ring_device((me + shift + n) % n, tp_size, cores_size).astype(jnp.int32)

    full_steps = (n - 1) // 2
    lefts, rights = [tokens], [tokens]
    for _ in range(1, full_steps + 1):
        lefts.append(lax.ppermute(lefts[-1], TP, forward))
        rights.append(lax.ppermute(rights[-1], TP, backward))
    last_top = lax.ppermute(lefts[-1][:half], TP, forward)
    last_bottom = lax.ppermute(rights[-1][half:], TP, backward)

    piece = depth // groups
    a = down_factor_pool.reshape(n // groups, groups, piece, twice_rank)
    a = lax.all_to_all(a, "grp", split_axis=1, concat_axis=0, tiled=True)
    a = a.reshape(n, piece, twice_rank)
    a = lax.all_to_all(a, TP, split_axis=0, concat_axis=0, tiled=True)
    b = up_factor_pool.reshape(up_factor_pool.shape[2:])
    b = lax.all_to_all(b, TP, split_axis=0, concat_axis=0, tiled=True)
    slots = jnp.take(adapter_pool_rows, segment_adapters.reshape(-1))
    a = jnp.take(a, slots, axis=0)
    b = jnp.take(b, slots, axis=0)
    a = lax.all_to_all(a, "grp", split_axis=0, concat_axis=0, tiled=True)
    b = lax.all_to_all(b, "grp", split_axis=0, concat_axis=0, tiled=True)
    a = a.reshape(groups, seg_count, piece, twice_rank)
    b = b.reshape(groups, seg_count, *b.shape[1:])
    block_cols = narrow
    if narrow % 128:
        block_cols = local_hidden_width
        b = b.reshape(groups, seg_count, b.shape[2], 2, narrow)
        b = jnp.transpose(b, (1, 2, 3, 0, 4))
        b = b.reshape(1, seg_count, b.shape[1], 2 * block_cols)

    tile_count = token_count // TILE
    tile_seg = tile_segments(segment_tile_counts[0], tile_count).astype(jnp.int32)
    row_seg = jnp.repeat(tile_seg, TILE)[:, None]
    partial = None
    for j in range(seg_count):
        term = jnp.dot(
            tokens, a[:, j].reshape(depth, twice_rank), preferred_element_type=jnp.float32
        )
        partial = term if partial is None else jnp.where(row_seg == j, term, partial)
    share = token_count // n
    partial = lax.all_to_all(
        partial.reshape(n, share, twice_rank), TP, split_axis=0, concat_axis=0, tiled=True
    )
    own = jnp.sum(partial, axis=0).astype(jnp.bfloat16)
    shrunk = lax.all_to_all(
        jnp.broadcast_to(own[None], (n, share, twice_rank)),
        TP,
        split_axis=0,
        concat_axis=0,
        tiled=True,
    ).reshape(token_count, twice_rank)

    acc = None
    for s in range(1, full_steps + 1):
        xs = [lefts[s], rights[s]]
        rows = [owner(-s), owner(s)]
        if s == 1:
            xs.insert(0, tokens)
            rows.insert(0, owner(0))
        acc = partial_matmul(xs, gate_up_weight, jnp.stack(rows), acc, block_cols)
    return final_matmul(
        last_top, last_bottom, gate_up_weight, jnp.stack([owner(n // 2)]), acc, shrunk, b, tile_seg
    )


def solution(mesh):
    return jax.shard_map(
        compute,
        mesh=mesh,
        in_specs=(
            P("grp", ("tp", "cores")),
            P(None, None, ("tp", "cores")),
            P(("tp", "cores"), "grp", None),
            P(("tp", "cores"), "grp", None, None, None),
            P(),
            P("grp", None),
            P(),
        ),
        out_specs=P("grp", ("tp", "cores")),
        check_vma=False,
    )
```

```python
import functools

import jax
import jax.numpy as jnp
from jax import lax
from jax.experimental import pallas as pl
from jax.experimental.pallas import tpu as pltpu
from jax.sharding import PartitionSpec as P


TILE = 128
VMEM_LIMIT = 60 * 1024 * 1024

adapter_scale = 0.5


TP = ("tp", "cores")


def tile_segments(tile_lengths, tile_count):
    bounds = jnp.cumsum(tile_lengths)
    positions = jnp.arange(tile_count, dtype=jnp.int32)
    return jnp.sum((bounds[None, :] <= positions[:, None]).astype(jnp.int32), axis=1)


def ring_device(position, tp_size, cores_size):
    c = position // tp_size
    t = position % tp_size
    t = t + (c % 2) * (tp_size - 1 - 2 * t)
    return t * cores_size + c


def ring_position(tp_index, cores_index, tp_size):
    t = tp_index + (cores_index % 2) * (tp_size - 1 - 2 * tp_index)
    return cores_index * tp_size + t


def partial_kernel(count, with_acc, rows_ref, *refs):
    xs, ws = refs[:count], refs[count : 2 * count]
    out = refs[-1]
    ws = [jnp.swapaxes(w[...], 0, 1) for w in ws]
    for h in range(2):
        total = refs[2 * count][h] if with_acc else None
        for x, w in zip(xs, ws):
            term = jnp.dot(x[...], w[h], preferred_element_type=jnp.float32)
            total = term if total is None else total + term
        out[h] = total


def partial_matmul(xs, weight, rows, acc, block_cols):
    count = len(xs)
    tokens, depth = xs[0].shape
    hidden = weight.shape[2]
    block_cols = min(block_cols, 256)
    in_specs = [pl.BlockSpec((tokens, depth), lambda j, r: (0, 0))] * count
    for k in range(count):
        in_specs.append(
            pl.BlockSpec((depth, 2, block_cols), lambda j, r, k=k: (r[k], 0, j))
        )
    acc_spec = pl.BlockSpec((2, tokens, block_cols), lambda j, r: (0, 0, j))
    operands = list(xs) + [weight] * count
    aliases = {}
    if acc is not None:
        in_specs.append(acc_spec)
        aliases = {1 + len(operands): 0}
        operands.append(acc)
    return pl.pallas_call(
        functools.partial(partial_kernel, count, acc is not None),
        out_shape=jax.ShapeDtypeStruct((2, tokens, hidden), jnp.float32),
        grid_spec=pltpu.PrefetchScalarGridSpec(
            num_scalar_prefetch=1,
            grid=(hidden // block_cols,),
            in_specs=in_specs,
            out_specs=acc_spec,
        ),
        input_output_aliases=aliases,
        compiler_params=pltpu.CompilerParams(vmem_limit_bytes=VMEM_LIMIT),
        cost_estimate=pl.CostEstimate(
            flops=4 * count * tokens * depth * hidden,
            bytes_accessed=count * 4 * depth * hidden + 16 * tokens * hidden,
            transcendentals=0,
        ),
    )(rows, *operands)


def final_kernel(tiles_per_half, rank, rows_ref, seg_ref, xt, xb, w, acc, shrunk, b, out, total):
    narrow = out.shape[1]
    w = jnp.swapaxes(w[...], 0, 1)
    for p, x in enumerate((xt, xb)):
        for h in range(2):
            span = slice(p * x.shape[0], (p + 1) * x.shape[0])
            total[h, span] = acc[h, span] + jnp.dot(
                x[...], w[h], preferred_element_type=jnp.float32
            )
        for t in range(p * tiles_per_half, (p + 1) * tiles_per_half):
            seg = seg_ref[t]
            span = slice(t * TILE, (t + 1) * TILE)
            both = []
            for h in range(2):
                delta = jnp.dot(
                    shrunk[span, h * rank : (h + 1) * rank],
                    b[0, seg, :, h * narrow : (h + 1) * narrow],
                    preferred_element_type=jnp.float32,
                )
                both.append(total[h, span] + adapter_scale * delta)
            gate, up = both
            out[span] = (gate / (1.0 + jnp.exp(-gate)) * up).astype(out.dtype)


def final_matmul(xt, xb, weight, rows, acc, shrunk, b_chosen, tile_seg):
    half, depth = xt.shape
    tokens = 2 * half
    hidden = weight.shape[2]
    blocks, segs, rank, twice = b_chosen.shape
    narrow = twice // 2
    return pl.pallas_call(
        functools.partial(final_kernel, half // TILE, rank),
        out_shape=jax.ShapeDtypeStruct((tokens, hidden), jnp.bfloat16),
        grid_spec=pltpu.PrefetchScalarGridSpec(
            num_scalar_prefetch=2,
            grid=(blocks,),
            in_specs=[
                pl.BlockSpec((half, depth), lambda j, r, s: (0, 0)),
                pl.BlockSpec((half, depth), lambda j, r, s: (0, 0)),
                pl.BlockSpec((depth, 2, narrow), lambda j, r, s: (r[0], 0, j)),
                pl.BlockSpec((2, tokens, narrow), lambda j, r, s: (0, 0, j)),
                pl.BlockSpec((tokens, 2 * rank), lambda j, r, s: (0, 0)),
                pl.BlockSpec((1, segs, rank, twice), lambda j, r, s: (j, 0, 0, 0)),
            ],
            out_specs=pl.BlockSpec((tokens, narrow), lambda j, r, s: (0, j)),
            scratch_shapes=[pltpu.VMEM((2, tokens, narrow), jnp.float32)],
        ),
        compiler_params=pltpu.CompilerParams(vmem_limit_bytes=VMEM_LIMIT),
        cost_estimate=pl.CostEstimate(
            flops=4 * tokens * (depth + rank) * hidden,
            bytes_accessed=4 * depth * hidden + 10 * tokens * hidden,
            transcendentals=tokens * hidden,
        ),
    )(rows, tile_seg, xt, xb, weight, acc, shrunk, b_chosen)


def group_exchange(pool, slots):
    groups = lax.axis_size("grp")
    g = lax.axis_index("grp")
    parts = []
    for k in range(groups):
        wanted = lax.dynamic_index_in_dim(slots, (g + k) % groups, 0, keepdims=False)
        part = jnp.take(pool, wanted, axis=0, mode="clip")
        if k:
            pairs = [(i, (i + k) % groups) for i in range(groups)]
            part = lax.ppermute(part, "grp", pairs)
        parts.append(part)
    sources = (g + groups - jnp.arange(groups)) % groups
    return jnp.take(jnp.stack(parts), sources, axis=0, mode="clip")


def compute(
    tokens,
    gate_up_weight,
    down_factor_pool,
    up_factor_pool,
    segment_adapters,
    segment_tile_counts,
    adapter_pool_rows,
):
    groups = lax.axis_size("grp")
    tp_size, cores_size = lax.axis_size("tp"), lax.axis_size("cores")
    n = tp_size * cores_size
    token_count, depth = tokens.shape
    local_hidden_width = gate_up_weight.shape[2]
    twice_rank = down_factor_pool.shape[2]
    narrow = local_hidden_width // groups
    seg_count = segment_adapters.shape[1]
    half = token_count // 2

    me = ring_position(lax.axis_index("tp"), lax.axis_index("cores"), tp_size)
    order = [ring_device(k, tp_size, cores_size) for k in range(n)]
    forward = [(order[k], order[(k + 1) % n]) for k in range(n)]
    backward = [(order[(k + 1) % n], order[k]) for k in range(n)]

    def owner(shift):
        return ring_device((me + shift + n) % n, tp_size, cores_size).astype(jnp.int32)

    full_steps = (n - 1) // 2
    lefts, rights = [tokens], [tokens]
    for _ in range(1, full_steps + 1):
        lefts.append(lax.ppermute(lefts[-1], TP, forward))
        rights.append(lax.ppermute(rights[-1], TP, backward))
    last_top = lax.ppermute(lefts[-1][:half], TP, forward)
    last_bottom = lax.ppermute(rights[-1][half:], TP, backward)

    piece = depth // groups
    a = down_factor_pool.reshape(n // groups, groups, piece, twice_rank)
    a = lax.all_to_all(a, "grp", split_axis=1, concat_axis=0, tiled=True)
    a = a.reshape(n, piece, twice_rank)
    a = lax.all_to_all(a, TP, split_axis=0, concat_axis=0, tiled=True)
    b = up_factor_pool.reshape(up_factor_pool.shape[2:])
    b = lax.all_to_all(b, TP, split_axis=0, concat_axis=0, tiled=True)
    slots = jnp.take(adapter_pool_rows, segment_adapters, mode="clip")
    a = group_exchange(a, slots)
    b = group_exchange(b, slots)
    block_cols = narrow
    if narrow % 128:
        block_cols = local_hidden_width
        b = b.reshape(groups, seg_count, b.shape[2], 2, narrow)
        b = jnp.transpose(b, (1, 2, 3, 0, 4))
        b = b.reshape(1, seg_count, b.shape[1], 2 * block_cols)

    tile_count = token_count // TILE
    tile_seg = tile_segments(segment_tile_counts[0], tile_count).astype(jnp.int32)
    row_seg = jnp.repeat(tile_seg, TILE)[:, None]
    partial = None
    for j in range(seg_count):
        term = jnp.dot(
            tokens, a[:, j].reshape(depth, twice_rank), preferred_element_type=jnp.float32
        )
        partial = term if partial is None else jnp.where(row_seg == j, term, partial)
    share = token_count // n
    partial = lax.all_to_all(
        partial.reshape(n, share, twice_rank), TP, split_axis=0, concat_axis=0, tiled=True
    )
    own = jnp.sum(partial, axis=0).astype(jnp.bfloat16)
    shrunk = lax.all_to_all(
        jnp.broadcast_to(own[None], (n, share, twice_rank)),
        TP,
        split_axis=0,
        concat_axis=0,
        tiled=True,
    ).reshape(token_count, twice_rank)

    acc = None
    for s in range(1, full_steps + 1):
        xs = [lefts[s], rights[s]]
        rows = [owner(-s), owner(s)]
        if s == 1:
            xs.insert(0, tokens)
            rows.insert(0, owner(0))
        acc = partial_matmul(xs, gate_up_weight, jnp.stack(rows), acc, block_cols)
    return final_matmul(
        last_top, last_bottom, gate_up_weight, jnp.stack([owner(n // 2)]), acc, shrunk, b, tile_seg
    )


def solution(mesh):
    return jax.shard_map(
        compute,
        mesh=mesh,
        in_specs=(
            P("grp", ("tp", "cores")),
            P(None, None, ("tp", "cores")),
            P(("tp", "cores"), "grp", None),
            P(("tp", "cores"), "grp", None, None, None),
            P(),
            P("grp", None),
            P(),
        ),
        out_specs=P("grp", ("tp", "cores")),
        check_vma=False,
    )
```
